1024 devices in a mesh: rows: 64 (over y, x, z_hi, core), depth: 16 (over z_lo).
Axes of the slice: x: 4, y: 4, z: 32 (z_hi: 2, z_lo: 16; z = z_hi * 16 + z_lo), core: 2. Of those that a mesh axis runs over, the one named last changes fastest.
Arguments:
- field: float32 [512, 256, 1024], P('rows', 'depth'), may hold values from 0 to 1
- diffusivity: bfloat16 [512, 256, 1024], P('rows', 'depth'), may hold values from 0.019897461 to 0.119628906
- velocity: bfloat16 [3, 512, 256, 1024], P(None, 'rows', 'depth'), may hold values from -1 to 1
Outputs:
- front: float32 [512, 256, 1024], P('rows', 'depth')
- picture: float32 [4, 512, 1024], P(None, 'rows', 'depth')
The draws below stay inside these ranges and needn't reach their ends.
All inputs are finite; a program needn't handle non-finite values.
Results may differ from the reference program's by a relative error of at most 0.0003.
Values sent between devices are 32-bit elements; how exact they have to be, the bound alone decides.
A program may use at most 32 MiB of HBM per device.

```python
import math
import jax
import jax.numpy as jnp
from jax import lax

NY = 1024
NX = 512
NZ = 256


def block_scale(own_key, shape, split, smallest, top_value):
    def one(axis_at, shards_of):
        draws = jax.random.uniform(jax.random.fold_in(jax.random.fold_in(own_key, 6), axis_at), (shards_of,), jnp.float32, smallest / len(split), top_value / len(split))
        return jnp.repeat(jnp.exp(draws), shape[axis_at] // shards_of).reshape((-1,) + (1,) * (len(shape) - axis_at - 1))

    gain = one(*split[0])
    for cut in split[1:]:
        gain = gain * one(*cut)
    return gain


def setup_inputs(seed: int = 0) -> dict:
    arg_keys = jax.random.split(jax.random.key(seed), 4)
    field = jnp.clip(1.0 * jax.random.uniform(arg_keys[0], (NX, NZ, NY), jnp.float32) ** block_scale(arg_keys[0], (NX, NZ, NY), ((0, 64), (1, 16)), -0.2, 0.2), 0.0, 1.0)
    diffusivity = jnp.clip(jnp.exp(math.log(0.119628906) - 1.7938024 * jax.random.uniform(arg_keys[1], (NX, NZ, NY), jnp.float32) ** block_scale(arg_keys[1], (NX, NZ, NY), ((0, 64), (1, 16)), -0.2, 0.2)), 0.019897461, 0.119628906).astype(jnp.bfloat16)
    velocity = jnp.clip(jax.random.uniform(arg_keys[2], (3, NX, NZ, NY), jnp.float32, -1.0, 1.0) * block_scale(arg_keys[2], (3, NX, NZ, NY), ((1, 64), (2, 16)), -0.4, 0.0), -1.0, 1.0).astype(jnp.bfloat16)
    return {"field": field, "diffusivity": diffusivity, "velocity": velocity}


time_step = 0.2
growth_rate = 1.0
opacity_total = 3.0


def upwind(speed, center, behind, ahead):
    return jnp.maximum(speed, 0.0) * (center - behind) + jnp.minimum(speed, 0.0) * (ahead - center)


def evolve(extended, diffusivity, velocity):
    padded = jnp.pad(extended, ((0, 0), (0, 0), (1, 1)))
    center = padded[1:-1, 1:-1, 1:-1]
    row_after = padded[2:, 1:-1, 1:-1]
    row_before = padded[:-2, 1:-1, 1:-1]
    deep_after = padded[1:-1, 2:, 1:-1]
    deep_before = padded[1:-1, :-2, 1:-1]
    col_after = padded[1:-1, 1:-1, 2:]
    col_before = padded[1:-1, 1:-1, :-2]
    laplace = row_after + row_before + deep_after + deep_before + col_after + col_before - 6.0 * center
    transport = upwind(velocity[0], center, row_before, row_after)
    transport = transport + upwind(velocity[1], center, deep_before, deep_after)
    transport = transport + upwind(velocity[2], center, col_before, col_after)
    return center + time_step * (diffusivity * laplace - transport + growth_rate * center * (1.0 - center))


def render(extended, opacity):
    padded = jnp.pad(extended, ((0, 0), (0, 0), (1, 1)))
    center = padded[1:-1, 1:-1, 1:-1]
    grad_row = (padded[2:, 1:-1, 1:-1] - padded[:-2, 1:-1, 1:-1]) * 0.5
    grad_deep = (padded[1:-1, 2:, 1:-1] - padded[1:-1, :-2, 1:-1]) * 0.5
    grad_col = (padded[1:-1, 1:-1, 2:] - padded[1:-1, 1:-1, :-2]) * 0.5
    lighting = 0.48 * grad_row + 0.64 * grad_deep + 0.6 * grad_col
    magnitude = grad_row * grad_row + grad_deep * grad_deep + grad_col * grad_col + 0.1
    shade = 0.35 + 0.65 * lighting * lighting / magnitude
    optical = opacity * center
    through = jnp.cumsum(optical, axis=1)
    weight = jnp.exp(optical - through) * (1.0 - jnp.exp(-optical)) * shade
    red = jnp.sum(weight * center, axis=1)
    green = jnp.sum(weight * center * center, axis=1)
    blue = jnp.sum(weight * (1.0 - center), axis=1)
    remain = jnp.exp(-through[:, -1])
    return jnp.stack([red, green, blue, remain])


def ref_section(field, diffusivity, velocity):
    padded = jnp.pad(field, ((1, 1), (1, 1), (0, 0)))
    row_block = math.gcd(NX, 8)

    def advance(block_index):
        first_row = block_index * row_block
        extended = lax.dynamic_slice_in_dim(padded, first_row, row_block + 2, 0)
        local_diff = lax.dynamic_slice_in_dim(diffusivity, first_row, row_block, 0).astype(jnp.float32)
        local_vel = lax.dynamic_slice_in_dim(velocity, first_row, row_block, 1).astype(jnp.float32)
        return evolve(extended, local_diff, local_vel)

    pieces = lax.map(advance, jnp.arange(NX // row_block, dtype=jnp.int32))
    return pieces.reshape(NX, NZ, NY)


def ref_render(front):
    padded = jnp.pad(front, ((1, 1), (1, 1), (0, 0)))
    row_block = math.gcd(NX, 8)

    def shine(block_index):
        first_row = block_index * row_block
        extended = lax.dynamic_slice_in_dim(padded, first_row, row_block + 2, 0)
        return render(extended, opacity_total / NZ)

    pieces = lax.map(shine, jnp.arange(NX // row_block, dtype=jnp.int32))
    return pieces.transpose(1, 0, 2, 3).reshape(4, NX, NY)


def reference(field, diffusivity, velocity):
    middle = ref_section(field, diffusivity, velocity)
    front = ref_section(middle, diffusivity, velocity)
    picture = ref_render(front)
    return front, picture
```

```python
import functools

import jax
import jax.numpy as jnp
from jax import lax
from jax.experimental import pallas as pl
from jax.experimental.pallas import tpu as pltpu
from jax.sharding import PartitionSpec as P

TIME_STEP = 0.2
OPACITY_TOTAL = 3.0
MESH = pl.DeviceIdType.MESH

(FAR_U, FAR_C, NEAR_U, LO_U, HI_U, NEAR_M, LO_M, HI_M, NEAR_F, FAR_M,
 LO_MB, HI_MB, FAR_P, LO_F, HI_F, LO_FB, HI_FB, COPIES) = range(18)


def shifted(value, before, axis, low, high):
    size = value.shape[axis]
    index = lax.broadcasted_iota(jnp.int32, value.shape, axis)
    if before:
        return jnp.where(index == 0, low, pltpu.roll(value, 1, axis))
    return jnp.where(index == size - 1, high, pltpu.roll(value, size - 1, axis))


def section(ref, low, high, diff, vel, i):
    center, row_before, row_after = ref[i + 1], ref[i], ref[i + 2]
    deep_before = shifted(center, True, 0, low[i], None)
    deep_after = shifted(center, False, 0, None, high[i])
    col_before = shifted(center, True, 1, 0.0, None)
    col_after = shifted(center, False, 1, None, 0.0)
    k = diff[i].astype(jnp.float32)
    total = 1.0 - 6.0 * k
    flow = None
    for dim, (back, ahead) in enumerate(
        ((row_before, row_after), (deep_before, deep_after), (col_before, col_after))
    ):
        speed = vel[dim, i].astype(jnp.float32)
        up, down = jnp.maximum(speed, 0.0), jnp.minimum(speed, 0.0)
        part = (k + up) * back + (k - down) * ahead
        flow = part if flow is None else flow + part
        total = total - (up - down)
    return center + TIME_STEP * (flow + center * (total - center))


def ray_row(ref, low, high, i, opacity):
    center = ref[i + 1]
    grad_row = (ref[i + 2] - ref[i]) * 0.5
    grad_deep = (shifted(center, False, 0, None, high[i]) - shifted(center, True, 0, low[i], None)) * 0.5
    grad_col = (shifted(center, False, 1, None, 0.0) - shifted(center, True, 1, 0.0, None)) * 0.5
    lighting = 0.48 * grad_row + 0.64 * grad_deep + 0.6 * grad_col
    magnitude = grad_row * grad_row + grad_deep * grad_deep + grad_col * grad_col + 0.1
    shade = 0.35 + 0.65 * lighting * lighting / magnitude
    optical = opacity * center
    size = center.shape[0]
    index = lax.broadcasted_iota(jnp.int32, center.shape, 0)
    through, step = optical, 1
    while step < size:
        through = through + jnp.where(index >= step, pltpu.roll(through, step, 0), 0.0)
        step *= 2
    weight = jnp.exp(optical - through) * (1.0 - jnp.exp(-optical)) * shade
    bright = weight * center
    red = jnp.sum(bright, axis=0, keepdims=True)
    green = jnp.sum(bright * center, axis=0, keepdims=True)
    blue = jnp.sum(weight - bright, axis=0, keepdims=True)
    return red, green, blue, jnp.exp(-through[size - 1 : size])


def kernel(rows, depths, opacity, field, diffusivity, velocity, front_out, picture, u, m, f, diff,
           vel, coef, far_u, far_c, far_m, far_p, p_row, lo, hi, edge_lo, edge_hi, lo_b, hi_b,
           edge_lo_b, edge_hi_b, part, comp, result, load, store, send, recv, send_a, recv_a):
    r, d = lax.axis_index("rows"), lax.axis_index("depth")
    core = r % 2
    count = field.shape[0]
    last = count - 1
    b = last * core
    inner = last - 1 - (last - 2) * (1 - core)
    near_row = last - b
    far_slot = (count + 1) * core
    first_free = 2 * (1 - core)
    near, far = r + 1 - 2 * core, r - 1 + 2 * core
    has_far = jnp.logical_and(far >= 0, far < rows)
    has_lo, has_hi = d > 0, d < depths - 1
    tiles = field.shape[2] // 128

    loads = [
        pltpu.make_async_copy(field, u.at[pl.ds(1, count)], load.at[0]),
        pltpu.make_async_copy(diffusivity, diff, load.at[1]),
        pltpu.make_async_copy(velocity, vel, load.at[2]),
    ]
    barrier = pltpu.get_barrier_semaphore()

    @pl.when(has_far)
    def _():
        pl.semaphore_signal(barrier, inc=1, device_id=(far, d), device_id_type=MESH)

    pl.semaphore_signal(barrier, inc=1, device_id=(near, d), device_id_type=MESH)

    def greet(k, carry):
        pl.semaphore_signal(
            barrier, inc=1, device_id=(r, lax.rem(d + k, depths)), device_id_type=MESH
        )
        return carry

    for copy in loads:
        copy.start()
    lax.fori_loop(1, depths, greet, 0)

    zero_row = jnp.zeros(u.shape[1:], jnp.float32)
    u[far_slot] = zero_row
    m[far_slot] = zero_row

    @pl.when(jnp.logical_not(has_far))
    def _():
        for ref in (far_u, far_c, far_m, far_p):
            ref[...] = zero_row

    @pl.when(jnp.logical_not(has_lo))
    def _():
        lo[...] = jnp.zeros_like(lo)
        lo_b[...] = jnp.zeros_like(lo_b)

    @pl.when(jnp.logical_not(has_hi))
    def _():
        hi[...] = jnp.zeros_like(hi)
        hi_b[...] = jnp.zeros_like(hi_b)

    for copy in loads:
        copy.wait()

    k = diff[b].astype(jnp.float32)
    speed = vel[0, b].astype(jnp.float32)
    coef[...] = TIME_STEP * (
        k + jnp.where(core == 1, -jnp.minimum(speed, 0.0), jnp.maximum(speed, 0.0))
    )

    def edges(i, stage, value):
        edge_lo[stage, i] = value[:1]
        edge_hi[stage, i] = value[-1:]

    def field_edges(i, carry):
        edges(i, 0, u[i + 1])
        return carry

    lax.fori_loop(0, count, field_edges, 0)

    pl.semaphore_wait(barrier, depths + has_far.astype(jnp.int32))

    def remote(name, src, dst, target):
        return pltpu.make_async_remote_copy(
            src_ref=src, dst_ref=dst, send_sem=send.at[name], recv_sem=recv.at[name],
            device_id=target, device_id_type=MESH,
        )

    far_copies = {
        FAR_U: remote(FAR_U, u.at[b + 1], far_u, (far, d)),
        FAR_C: remote(FAR_C, coef, far_c, (far, d)),
        FAR_M: remote(FAR_M, m.at[b + 1], far_m, (far, d)),
        FAR_P: remote(FAR_P, p_row, far_p, (far, d)),
    }
    near_slot = (count + 1) * core
    near_copies = {
        name: remote(name, ref.at[near_row + 1], ref.at[near_slot], (near, d))
        for name, ref in ((NEAR_U, u), (NEAR_M, m), (NEAR_F, f))
    }
    lo_copies = {
        name: remote(name, src, dst, (r, d - 1))
        for name, src, dst in (
            (LO_U, edge_lo.at[0], hi.at[0]), (LO_M, edge_lo.at[1], hi.at[1]),
            (LO_F, edge_lo.at[2], hi.at[2]), (LO_MB, edge_lo_b.at[0], hi_b.at[0]),
            (LO_FB, edge_lo_b.at[1], hi_b.at[1]),
        )
    }
    hi_copies = {
        name: remote(name, src, dst, (r, d + 1))
        for name, src, dst in (
            (HI_U, edge_hi.at[0], lo.at[0]), (HI_M, edge_hi.at[1], lo.at[1]),
            (HI_F, edge_hi.at[2], lo.at[2]), (HI_MB, edge_hi_b.at[0], lo_b.at[0]),
            (HI_FB, edge_hi_b.at[1], lo_b.at[1]),
        )
    }

    def send_deep(to_lo, to_hi):
        @pl.when(has_lo)
        def _():
            lo_copies[to_lo].start()

        @pl.when(has_hi)
        def _():
            hi_copies[to_hi].start()

    def wait_deep(to_lo, to_hi):
        @pl.when(has_hi)
        def _():
            lo_copies[to_lo].wait_recv()

        @pl.when(has_lo)
        def _():
            hi_copies[to_hi].wait_recv()

    @pl.when(has_far)
    def _():
        far_copies[FAR_U].start()

    near_copies[NEAR_U].start()
    send_deep(LO_U, HI_U)

    @pl.when(has_far)
    def _():
        far_copies[FAR_C].start()

    near_copies[NEAR_U].wait_recv()
    wait_deep(LO_U, HI_U)

    def first(i, carry):
        value = section(u, lo.at[0], hi.at[0], diff, vel, i)
        m[i + 1] = value
        edges(i, 1, value)
        return carry

    lax.fori_loop(0, count, first, 0)
    near_copies[NEAR_M].start()
    send_deep(LO_M, HI_M)
    near_copies[NEAR_M].wait_recv()
    wait_deep(LO_M, HI_M)

    def second(i, carry):
        value = section(m, lo.at[1], hi.at[1], diff, vel, i)
        f[i + 1] = value
        edges(i, 2, value)
        return carry

    lax.fori_loop(first_free, first_free + count - 2, second, 0)
    near_copies[NEAR_F].start()

    @pl.when(has_far)
    def _():
        far_copies[FAR_U].wait_recv()

    value = m[b + 1] + coef[...] * far_u[...]
    m[b + 1] = value
    edge_lo_b[0] = value[:1]
    edge_hi_b[0] = value[-1:]
    send_deep(LO_MB, HI_MB)

    @pl.when(has_far)
    def _():
        far_copies[FAR_M].start()

    wait_deep(LO_MB, HI_MB)
    lo[1, b] = lo_b[0]
    hi[1, b] = hi_b[0]
    value = section(m, lo.at[1], hi.at[1], diff, vel, b)
    p_row[...] = value

    @pl.when(has_far)
    def _():
        far_copies[FAR_P].start()

    edges(b, 2, value)
    second(inner, 0)
    send_deep(LO_F, HI_F)
    near_copies[NEAR_F].wait_recv()
    wait_deep(LO_F, HI_F)

    def pair(p, carry):
        low, high = lo.at[2], hi.at[2]
        one = ray_row(f, low, high, 2 * p, opacity)
        two = ray_row(f, low, high, 2 * p + 1, opacity)
        both = jnp.concatenate([x for v in zip(one, two) for x in v], axis=0)
        for j in range(tiles):
            part[j, p] = both[:, j * 128 : (j + 1) * 128]
        return carry

    pairs = count // 2
    early = pl.ds(1 - core, pairs - 1)
    late_pair = (pairs - 1) * core
    lax.fori_loop(1 - core, pairs - core, pair, 0)

    def spread(stage, span, k):
        target = lax.rem(d + k, depths)
        return pltpu.make_async_remote_copy(
            src_ref=part.at[target // 2, span], dst_ref=comp.at[d, span],
            send_sem=send_a.at[stage, k], recv_sem=recv_a.at[stage, d],
            device_id=(r, target), device_id_type=MESH,
        )

    def arrived(stage, span, k):
        source = lax.rem(d + k, depths)
        pltpu.make_async_remote_copy(
            src_ref=part.at[0, span], dst_ref=comp.at[source, span],
            send_sem=send_a.at[stage, k], recv_sem=recv_a.at[stage, source],
            device_id=(r, source), device_id_type=MESH,
        ).wait_recv()

    def start_spread(stage, span):
        def body(k, carry):
            spread(stage, span, k).start()
            return carry

        lax.fori_loop(1, depths, body, 0)

    def end_spread(stage, span):
        def body(k, carry):
            arrived(stage, span, k)
            return carry

        lax.fori_loop(1, depths, body, 0)

    start_spread(0, early)

    @pl.when(has_far)
    def _():
        far_copies[FAR_M].wait_recv()

    value = p_row[...] + coef[...] * far_m[...]
    f[b + 1] = value
    edge_lo_b[1] = value[:1]
    edge_hi_b[1] = value[-1:]
    send_deep(LO_FB, HI_FB)
    write = pltpu.make_async_copy(f.at[pl.ds(1, count)], front_out, store.at[0])
    write.start()

    @pl.when(has_far)
    def _():
        far_copies[FAR_C].wait_recv()
        far_copies[FAR_P].wait_recv()

    f[far_slot] = far_p[...] + far_c[...] * m[b + 1]
    wait_deep(LO_FB, HI_FB)
    lo[2, b] = lo_b[1]
    hi[2, b] = hi_b[1]
    pair(late_pair, 0)
    late = pl.ds(late_pair, 1)
    start_spread(1, late)
    for p in range(pairs):
        comp[d, p] = part[d // 2, p]

    def composite(p, carry):
        total = jnp.zeros((6, 128), jnp.float32)
        clear = jnp.ones((2, 128), jnp.float32)
        for s in range(depths):
            block = comp[s, p]
            total = total + jnp.concatenate([clear] * 3, axis=0) * block[:6]
            clear = clear * block[6:]
        tile = jnp.concatenate([total, clear], axis=0)
        result[p] = jnp.where(d % 2 == 0, tile, pltpu.roll(tile, 64, 1))
        return carry

    end_spread(0, early)
    lax.fori_loop(1 - core, pairs - core, composite, 0)
    end_spread(1, late)
    composite(late_pair, 0)
    for p in range(pairs):
        tile = result[p]
        for v in range(4):
            picture[v, 2 * p : 2 * p + 2] = tile[2 * v : 2 * v + 2, : picture.shape[2]]

    for name in near_copies:
        near_copies[name].wait_send()

    @pl.when(has_far)
    def _():
        for name in far_copies:
            far_copies[name].wait_send()

    @pl.when(has_lo)
    def _():
        for name in lo_copies:
            lo_copies[name].wait_send()

    @pl.when(has_hi)
    def _():
        for name in hi_copies:
            hi_copies[name].wait_send()

    def sent(k, carry):
        spread(0, early, k).wait_send()
        spread(1, late, k).wait_send()
        return carry

    lax.fori_loop(1, depths, sent, 0)
    write.wait()


def shards(rows, depths, field, diffusivity, velocity):
    count, deep, width = field.shape
    row = (deep, width)
    f32 = jnp.float32
    tiles, pairs = width // 128, count // 2
    any_space = pl.BlockSpec(memory_space=pl.ANY)
    vmem = pltpu.VMEM
    return pl.pallas_call(
        functools.partial(kernel, rows, depths, OPACITY_TOTAL / (deep * depths)),
        out_shape=(
            jax.ShapeDtypeStruct(field.shape, f32),
            jax.ShapeDtypeStruct((4, count, width // depths), f32),
        ),
        in_specs=[any_space] * 3,
        out_specs=(any_space, pl.BlockSpec(memory_space=pltpu.VMEM)),
        scratch_shapes=[
            vmem((count + 2,) + row, f32),
            vmem((count + 2,) + row, f32),
            vmem((count + 2,) + row, f32),
            vmem(diffusivity.shape, diffusivity.dtype),
            vmem(velocity.shape, velocity.dtype),
            vmem(row, f32), vmem(row, f32), vmem(row, f32), vmem(row, f32), vmem(row, f32), vmem(row, f32),
            vmem((3, count, 1, width), f32), vmem((3, count, 1, width), f32),
            vmem((3, count, 1, width), f32), vmem((3, count, 1, width), f32),
            vmem((2, 1, width), f32), vmem((2, 1, width), f32),
            vmem((2, 1, width), f32), vmem((2, 1, width), f32),
            vmem((tiles, pairs, 8, 128), f32),
            vmem((depths, pairs, 8, 128), f32),
            vmem((pairs, 8, 128), f32),
            pltpu.SemaphoreType.DMA((3,)),
            pltpu.SemaphoreType.DMA((1,)),
            pltpu.SemaphoreType.DMA((COPIES,)),
            pltpu.SemaphoreType.DMA((COPIES,)),
            pltpu.SemaphoreType.DMA((2, depths)),
            pltpu.SemaphoreType.DMA((2, depths)),
        ],
        compiler_params=pltpu.CompilerParams(collective_id=0, has_side_effects=True),
        name="front_and_rays",
    )(field, diffusivity, velocity)


def solution(mesh):
    return jax.shard_map(
        functools.partial(shards, mesh.shape["rows"], mesh.shape["depth"]),
        mesh=mesh,
        in_specs=(
            P("rows", "depth", None),
            P("rows", "depth", None),
            P(None, "rows", "depth", None),
        ),
        out_specs=(P("rows", "depth", None), P(None, "rows", "depth")),
        check_vma=False,
    )
```

```python
import functools

import jax
import jax.numpy as jnp
from jax import lax
from jax.experimental import pallas as pl
from jax.experimental.pallas import tpu as pltpu
from jax.sharding import PartitionSpec as P

TIME_STEP = 0.2
OPACITY_TOTAL = 3.0
MESH = pl.DeviceIdType.MESH

(NEAR_U, LO_U, HI_U, NEAR_M, LO_M, HI_M, NEAR_F, LO_F, HI_F,
 LO_MB, HI_MB, LO_FB, HI_FB, FAR_U) = range(14)
SPLIT = 2
CHUNKS = 2 * SPLIT
FAR_M, FAR_F = FAR_U + CHUNKS, FAR_U + 2 * CHUNKS
COPIES = FAR_U + 3 * CHUNKS


def shifted(value, before, axis, low, high):
    size = value.shape[axis]
    index = lax.broadcasted_iota(jnp.int32, value.shape, axis)
    if before:
        return jnp.where(index == 0, low, pltpu.roll(value, 1, axis))
    return jnp.where(index == size - 1, high, pltpu.roll(value, size - 1, axis))


def section(ref, low, high, diff, vel, i):
    center, row_before, row_after = ref[i + 1], ref[i], ref[i + 2]
    deep_before = shifted(center, True, 0, low[i], None)
    deep_after = shifted(center, False, 0, None, high[i])
    col_before = shifted(center, True, 1, 0.0, None)
    col_after = shifted(center, False, 1, None, 0.0)
    k = diff[i].astype(jnp.float32)
    total = 1.0 - 6.0 * k
    flow = None
    for dim, (back, ahead) in enumerate(
        ((row_before, row_after), (deep_before, deep_after), (col_before, col_after))
    ):
        speed = vel[dim, i].astype(jnp.float32)
        up, down = jnp.maximum(speed, 0.0), jnp.minimum(speed, 0.0)
        part = (k + up) * back + (k - down) * ahead
        flow = part if flow is None else flow + part
        total = total - (up - down)
    return center + TIME_STEP * (flow + center * (total - center))


def ray_row(ref, low, high, i, opacity):
    center = ref[i + 1]
    grad_row = (ref[i + 2] - ref[i]) * 0.5
    grad_deep = (shifted(center, False, 0, None, high[i]) - shifted(center, True, 0, low[i], None)) * 0.5
    grad_col = (shifted(center, False, 1, None, 0.0) - shifted(center, True, 1, 0.0, None)) * 0.5
    lighting = 0.48 * grad_row + 0.64 * grad_deep + 0.6 * grad_col
    magnitude = grad_row * grad_row + grad_deep * grad_deep + grad_col * grad_col + 0.1
    shade = 0.35 + 0.65 * lighting * lighting / magnitude
    optical = opacity * center
    size = center.shape[0]
    index = lax.broadcasted_iota(jnp.int32, center.shape, 0)
    through, step = optical, 1
    while step < size:
        through = through + jnp.where(index >= step, pltpu.roll(through, step, 0), 0.0)
        step *= 2
    weight = jnp.exp(optical - through) * (1.0 - jnp.exp(-optical)) * shade
    bright = weight * center
    red = jnp.sum(bright, axis=0, keepdims=True)
    green = jnp.sum(bright * center, axis=0, keepdims=True)
    blue = jnp.sum(weight - bright, axis=0, keepdims=True)
    return red, green, blue, jnp.exp(-through[size - 1 : size])


def kernel(rows, depths, opacity, field, diffusivity, velocity, front_out, picture, u, m, f, diff,
           vel, coef, far_u, far_m, p_row, lo, hi, edge_lo, edge_hi, lo_b, hi_b,
           edge_lo_b, edge_hi_b, part, comp, result, load, store, send, recv, send_a, recv_a, token):
    r, d = lax.axis_index("rows"), lax.axis_index("depth")
    core = r % 2
    count = field.shape[0]
    last = count - 1
    b = last * core
    inner = last - 1 - (last - 2) * (1 - core)
    near_row = last - b
    far_slot = (count + 1) * core
    first_free = 2 * (1 - core)
    near, far = r + 1 - 2 * core, r - 1 + 2 * core
    has_far = jnp.logical_and(far >= 0, far < rows)
    has_lo, has_hi = d > 0, d < depths - 1
    upper = r // 2 % 2 == 1
    tiles = field.shape[2] // 128

    loads = [
        pltpu.make_async_copy(field, u.at[pl.ds(1, count)], load.at[0]),
        pltpu.make_async_copy(diffusivity, diff, load.at[1]),
        pltpu.make_async_copy(velocity, vel, load.at[2]),
    ]
    barrier = pltpu.get_barrier_semaphore()

    @pl.when(has_far)
    def _():
        pl.semaphore_signal(barrier, inc=1, device_id=(far, d), device_id_type=MESH)

    pl.semaphore_signal(barrier, inc=1, device_id=(near, d), device_id_type=MESH)

    for there, target in ((has_lo, d - 1), (has_hi, d + 1)):
        @pl.when(there)
        def _():
            pl.semaphore_signal(barrier, inc=1, device_id=(r, target), device_id_type=MESH)

    for copy in loads:
        copy.start()

    zero_row = jnp.zeros(u.shape[1:], jnp.float32)
    u[far_slot] = zero_row
    m[far_slot] = zero_row

    @pl.when(jnp.logical_not(has_far))
    def _():
        far_u[...] = zero_row
        far_m[...] = zero_row
        f[far_slot] = zero_row

    @pl.when(jnp.logical_not(has_lo))
    def _():
        lo[...] = jnp.zeros_like(lo)
        lo_b[...] = jnp.zeros_like(lo_b)

    @pl.when(jnp.logical_not(has_hi))
    def _():
        hi[...] = jnp.zeros_like(hi)
        hi_b[...] = jnp.zeros_like(hi_b)

    for copy in loads:
        copy.wait()

    k = diff[b].astype(jnp.float32)
    speed = vel[0, b].astype(jnp.float32)
    coef[...] = TIME_STEP * (
        k + jnp.where(core == 1, -jnp.minimum(speed, 0.0), jnp.maximum(speed, 0.0))
    )

    def edges(i, stage, value):
        edge_lo[stage, i] = value[:1]
        edge_hi[stage, i] = value[-1:]

    def field_edges(i, carry):
        edges(i, 0, u[i + 1])
        return carry

    lax.fori_loop(0, count, field_edges, 0)

    pl.semaphore_wait(barrier, 1 + sum(x.astype(jnp.int32) for x in (has_far, has_lo, has_hi)))

    def remote(name, src, dst, target):
        return pltpu.make_async_remote_copy(
            src_ref=src, dst_ref=dst, send_sem=send.at[name], recv_sem=recv.at[name],
            device_id=target, device_id_type=MESH,
        )

    deep, wide = u.shape[1] // 2, u.shape[2] // SPLIT
    chunk = [
        (pl.ds(deep * p, deep), pl.ds(wide * q, wide)) for q in range(SPLIT) for p in range(2)
    ]
    far_copies = {}
    for h, at in enumerate(chunk):
        for name, src, dst in (
            (FAR_U, u.at[(b + 1,) + at], far_u.at[at]),
            (FAR_M, m.at[(b + 1,) + at], far_m.at[at]),
            (FAR_F, f.at[(b + 1,) + at], f.at[((count + 1) * (1 - core),) + at]),
        ):
            far_copies[name + h] = remote(name + h, src, dst, (far, d))
    near_slot = (count + 1) * core
    near_copies = {
        name: remote(name, ref.at[near_row + 1], ref.at[near_slot], (near, d))
        for name, ref in ((NEAR_U, u), (NEAR_M, m), (NEAR_F, f))
    }
    lo_copies = {
        name: remote(name, src, dst, (r, d - 1))
        for name, src, dst in (
            (LO_U, edge_lo.at[0], hi.at[0]), (LO_M, edge_lo.at[1], hi.at[1]),
            (LO_F, edge_lo.at[2], hi.at[2]), (LO_MB, edge_lo_b.at[0, 0], hi_b.at[0, 0]),
            (LO_FB, edge_lo_b.at[1], hi_b.at[1]),
        )
    }
    hi_copies = {
        name: remote(name, src, dst, (r, d + 1))
        for name, src, dst in (
            (HI_U, edge_hi.at[0], lo.at[0]), (HI_M, edge_hi.at[1], lo.at[1]),
            (HI_F, edge_hi.at[2], lo.at[2]), (HI_MB, edge_hi_b.at[0, 0], lo_b.at[0, 0]),
            (HI_FB, edge_hi_b.at[1], lo_b.at[1]),
        )
    }

    started = {}

    def start_far(name):
        started[name] = far_copies[name], has_far

        @pl.when(has_far)
        def _():
            far_copies[name].start()

    def wait_far(name):
        @pl.when(has_far)
        def _():
            far_copies[name].wait_recv()

    def start_near(name):
        started[name] = near_copies[name], None
        near_copies[name].start()

    def wait_near(name):
        near_copies[name].wait_recv()

    def start_deep(to_lo=None, to_hi=None):
        if to_lo is not None:
            started[to_lo] = lo_copies[to_lo], has_lo
            pl.when(has_lo)(lo_copies[to_lo].start)
        if to_hi is not None:
            started[to_hi] = hi_copies[to_hi], has_hi
            pl.when(has_hi)(hi_copies[to_hi].start)

    def wait_deep(to_lo, to_hi):
        pl.when(has_hi)(lo_copies[to_lo].wait_recv)
        pl.when(has_lo)(hi_copies[to_hi].wait_recv)

    start_deep(LO_U, HI_U)
    start_near(NEAR_U)
    for h in range(CHUNKS):
        start_far(FAR_U + h)
    wait_near(NEAR_U)
    wait_deep(LO_U, HI_U)

    def first(i, carry):
        value = section(u, lo.at[0], hi.at[0], diff, vel, i)
        m[i + 1] = value
        edges(i, 1, value)
        return carry

    lax.fori_loop(0, count, first, 0)
    start_deep(LO_M, HI_M)
    start_near(NEAR_M)
    wait_near(NEAR_M)
    wait_deep(LO_M, HI_M)

    def line_entered():
        for way, there, on, onward in ((0, has_lo, has_hi, d + 1), (1, has_hi, has_lo, d - 1)):
            @pl.when(there)
            def _():
                pl.semaphore_wait(token.at[way], 1)

            @pl.when(on)
            def _():
                pl.semaphore_signal(
                    token.at[way], inc=1, device_id=(r, onward), device_id_type=MESH
                )

    pl.when(upper)(line_entered)

    for h, at in enumerate(chunk):
        wait_far(FAR_U + h)
        here = (b + 1,) + at
        m[here] = m[here] + coef[at] * far_u[at]
        if h == CHUNKS - 1:
            edge_lo_b[0, 0] = m[b + 1, :1]
            edge_hi_b[0, 0] = m[b + 1, u.shape[1] - 1 :]
            start_deep(LO_MB, HI_MB)
        start_far(FAR_M + h)
    wait_deep(LO_MB, HI_MB)
    lo[1, b] = lo_b[0, 0]
    hi[1, b] = hi_b[0, 0]
    p_row[...] = section(m, lo.at[1], hi.at[1], diff, vel, b)

    def second(i, carry):
        value = section(m, lo.at[1], hi.at[1], diff, vel, i)
        f[i + 1] = value
        edges(i, 2, value)
        return carry

    def pair(p, carry):
        low, high = lo.at[2], hi.at[2]
        one, two = (
            jnp.concatenate(ray_row(f, low, high, 2 * p + q, opacity), axis=0) for q in range(2)
        )
        left = lax.broadcasted_iota(jnp.int32, (4, 128), 1) < 64
        for j in range(tiles):
            x, y = one[:, j * 128 : (j + 1) * 128], two[:, j * 128 : (j + 1) * 128]
            part[2 * j, p] = jnp.where(left, x, pltpu.roll(y, 64, 1))
            part[2 * j + 1, p] = jnp.where(left, pltpu.roll(x, 64, 1), y)
        return carry

    pairs = count // 2
    groups = pl.ds(1 - core, pairs - 1), pl.ds((pairs - 1) * core, 1)

    def spread(stage, k):
        target = lax.rem(d + k, depths)
        return pltpu.make_async_remote_copy(
            src_ref=part.at[target, groups[stage]], dst_ref=comp.at[d, groups[stage]],
            send_sem=send_a.at[stage, k], recv_sem=recv_a.at[stage, d],
            device_id=(r, target), device_id_type=MESH,
        )

    def start_spread(stage):
        def body(k, carry):
            spread(stage, k).start()
            return carry

        lax.fori_loop(1, depths, body, 0)

    def end_spread(stage):
        def body(k, carry):
            source = lax.rem(d + k, depths)
            pltpu.make_async_remote_copy(
                src_ref=part.at[0, groups[stage]], dst_ref=comp.at[source, groups[stage]],
                send_sem=send_a.at[stage, k], recv_sem=recv_a.at[stage, source],
                device_id=(r, source), device_id_type=MESH,
            ).wait_recv()
            return carry

        lax.fori_loop(1, depths, body, 0)

    def early_images():
        lax.fori_loop(first_free, first_free + count - 2, second, 0)
        start_deep(LO_F, HI_F)
        start_near(NEAR_F)
        value = section(m, lo.at[1], hi.at[1], diff, vel, inner)
        f[inner + 1] = value
        edge_lo_b[1, 1] = value[:1]
        edge_hi_b[1, 1] = value[-1:]
        pl.when(jnp.logical_not(upper))(line_entered)
        wait_near(NEAR_F)
        wait_deep(LO_F, HI_F)
        lax.fori_loop(1 - core, pairs - core, pair, 0)
        start_spread(0)

    pl.when(jnp.logical_not(upper))(early_images)
    for h, at in enumerate(chunk):
        wait_far(FAR_M + h)
        f[(b + 1,) + at] = p_row[at] + coef[at] * far_m[at]
        start_far(FAR_F + h)
    pl.when(upper)(early_images)
    edge_lo_b[1, 0] = f[b + 1, :1]
    edge_hi_b[1, 0] = f[b + 1, u.shape[1] - 1 :]
    start_deep(LO_FB, HI_FB)
    write = pltpu.make_async_copy(f.at[pl.ds(1, count)], front_out, store.at[0])
    write.start()
    wait_deep(LO_FB, HI_FB)
    for q, i in enumerate((b, inner)):
        lo[2, i] = lo_b[1, q]
        hi[2, i] = hi_b[1, q]
    for h in range(CHUNKS):
        wait_far(FAR_F + h)
    pair((pairs - 1) * core, 0)
    start_spread(1)
    comp[d] = part[d]

    def composite(p, carry):
        total = jnp.zeros((3, 128), jnp.float32)
        clear = jnp.ones((1, 128), jnp.float32)
        for s in range(depths):
            block = comp[s, p]
            total = total + clear * block[:3]
            clear = clear * block[3:]
        result[p] = jnp.concatenate([total, clear], axis=0)
        return carry

    end_spread(0)
    lax.fori_loop(1 - core, pairs - core, composite, 0)
    end_spread(1)
    composite((pairs - 1) * core, 0)
    for p in range(pairs):
        tile = result[p]
        other = pltpu.roll(tile, 64, 1)
        for v in range(4):
            picture[v, 2 * p : 2 * p + 1] = tile[v : v + 1, :64]
            picture[v, 2 * p + 1 : 2 * p + 2] = other[v : v + 1, :64]

    for copy, there in started.values():
        if there is None:
            copy.wait_send()
        else:
            pl.when(there)(copy.wait_send)

    def sent(k, carry):
        for stage in range(2):
            spread(stage, k).wait_send()
        return carry

    lax.fori_loop(1, depths, sent, 0)
    write.wait()


def shards(rows, depths, field, diffusivity, velocity):
    count, deep, width = field.shape
    row = (deep, width)
    f32 = jnp.float32
    pairs = count // 2
    any_space = pl.BlockSpec(memory_space=pl.ANY)
    vmem = pltpu.VMEM
    return pl.pallas_call(
        functools.partial(kernel, rows, depths, OPACITY_TOTAL / (deep * depths)),
        out_shape=(
            jax.ShapeDtypeStruct(field.shape, f32),
            jax.ShapeDtypeStruct((4, count, width // depths), f32),
        ),
        in_specs=[any_space] * 3,
        out_specs=(any_space, pl.BlockSpec(memory_space=pltpu.VMEM)),
        scratch_shapes=[
            vmem((count + 2,) + row, f32),
            vmem((count + 2,) + row, f32),
            vmem((count + 2,) + row, f32),
            vmem(diffusivity.shape, diffusivity.dtype),
            vmem(velocity.shape, velocity.dtype),
            vmem(row, f32), vmem(row, f32), vmem(row, f32), vmem(row, f32),
            vmem((3, count, 1, width), f32), vmem((3, count, 1, width), f32),
            vmem((3, count, 1, width), f32), vmem((3, count, 1, width), f32),
            vmem((2, 2, 1, width), f32), vmem((2, 2, 1, width), f32),
            vmem((2, 2, 1, width), f32), vmem((2, 2, 1, width), f32),
            vmem((depths, pairs, 4, 128), f32),
            vmem((depths, pairs, 4, 128), f32),
            vmem((pairs, 4, 128), f32),
            pltpu.SemaphoreType.DMA((3,)),
            pltpu.SemaphoreType.DMA((1,)),
            pltpu.SemaphoreType.DMA((COPIES,)),
            pltpu.SemaphoreType.DMA((COPIES,)),
            pltpu.SemaphoreType.DMA((2, depths)),
            pltpu.SemaphoreType.DMA((2, depths)),
            pltpu.SemaphoreType.REGULAR((2,)),
        ],
        compiler_params=pltpu.CompilerParams(collective_id=0, has_side_effects=True),
        name="front_and_rays",
    )(field, diffusivity, velocity)


def solution(mesh):
    return jax.shard_map(
        functools.partial(shards, mesh.shape["rows"], mesh.shape["depth"]),
        mesh=mesh,
        in_specs=(
            P("rows", "depth", None),
            P("rows", "depth", None),
            P(None, "rows", "depth", None),
        ),
        out_specs=(P("rows", "depth", None), P(None, "rows", "depth")),
        check_vma=False,
    )
```

```python
import functools

import jax
import jax.numpy as jnp
from jax import lax
from jax.experimental import pallas as pl
from jax.experimental.pallas import tpu as pltpu
from jax.sharding import PartitionSpec as P

TIME_STEP = 0.2
OPACITY_TOTAL = 3.0
MESH = pl.DeviceIdType.MESH

(NEAR_U, LO_U, HI_U, NEAR_M, LO_M, HI_M, NEAR_F, LO_F, HI_F,
 LO_MB, HI_MB, LO_FB, HI_FB, FAR_U) = range(14)
SPLIT = 4
CHUNKS = 2 * SPLIT
FAR_M, FAR_F = FAR_U + CHUNKS, FAR_U + 2 * CHUNKS
COPIES = FAR_U + 3 * CHUNKS

def shifted(value, before, axis, low, high):
    size = value.shape[axis]
    index = lax.broadcasted_iota(jnp.int32, value.shape, axis)
    if before:
        return jnp.where(index == 0, low, pltpu.roll(value, 1, axis))
    return jnp.where(index == size - 1, high, pltpu.roll(value, size - 1, axis))

def section(ref, low, high, diff, vel, i):
    center, row_before, row_after = ref[i + 1], ref[i], ref[i + 2]
    deep_before = shifted(center, True, 0, low[i], None)
    deep_after = shifted(center, False, 0, None, high[i])
    col_before = shifted(center, True, 1, 0.0, None)
    col_after = shifted(center, False, 1, None, 0.0)
    k = diff[i].astype(jnp.float32)
    total = 1.0 - 6.0 * k
    flow = None
    for dim, (back, ahead) in enumerate(
        ((row_before, row_after), (deep_before, deep_after), (col_before, col_after))
    ):
        speed = vel[dim, i].astype(jnp.float32)
        up, down = jnp.maximum(speed, 0.0), jnp.minimum(speed, 0.0)
        part = (k + up) * back + (k - down) * ahead
        flow = part if flow is None else flow + part
        total = total - (up - down)
    return center + TIME_STEP * (flow + center * (total - center))

def ray_row(ref, low, high, i, opacity):
    center = ref[i + 1]
    grad_row = (ref[i + 2] - ref[i]) * 0.5
    grad_deep = (shifted(center, False, 0, None, high[i]) - shifted(center, True, 0, low[i], None)) * 0.5
    grad_col = (shifted(center, False, 1, None, 0.0) - shifted(center, True, 1, 0.0, None)) * 0.5
    lighting = 0.48 * grad_row + 0.64 * grad_deep + 0.6 * grad_col
    magnitude = grad_row * grad_row + grad_deep * grad_deep + grad_col * grad_col + 0.1
    shade = 0.35 + 0.65 * lighting * lighting / magnitude
    optical = opacity * center
    size = center.shape[0]
    index = lax.broadcasted_iota(jnp.int32, center.shape, 0)
    through, step = optical, 1
    while step < size:
        through = through + jnp.where(index >= step, pltpu.roll(through, step, 0), 0.0)
        step *= 2
    weight = jnp.exp(optical - through) * (1.0 - jnp.exp(-optical)) * shade
    bright = weight * center
    red = jnp.sum(bright, axis=0, keepdims=True)
    green = jnp.sum(bright * center, axis=0, keepdims=True)
    blue = jnp.sum(weight - bright, axis=0, keepdims=True)
    return red, green, blue, jnp.exp(-through[size - 1 : size])

def kernel(rows, depths, opacity, field, diffusivity, velocity, front_out, picture, u, m, f, diff,
           vel, coef, far_u, far_m, p_row, lo, hi, edge_lo, edge_hi, lo_b, hi_b,
           edge_lo_b, edge_hi_b, part, comp, result, load, send, recv, send_a, recv_a, token):
    r, d = lax.axis_index("rows"), lax.axis_index("depth")
    core = r % 2
    count = field.shape[0]
    last = count - 1
    b = last * core
    inner = last - 1 - (last - 2) * (1 - core)
    near_row = last - b
    far_slot = (count + 1) * core
    first_free = 2 * (1 - core)
    near, far = r + 1 - 2 * core, r - 1 + 2 * core
    has_far = jnp.logical_and(far >= 0, far < rows)
    has_lo, has_hi = d > 0, d < depths - 1
    upper = r // 2 % 2 == 1
    tiles = field.shape[2] // 128

    loads = [
        pltpu.make_async_copy(field, u.at[pl.ds(1, count)], load.at[0]),
        pltpu.make_async_copy(diffusivity, diff, load.at[1]),
        pltpu.make_async_copy(velocity, vel, load.at[2]),
    ]
    barrier = pltpu.get_barrier_semaphore()

    @pl.when(has_far)
    def _():
        pl.semaphore_signal(barrier, inc=1, device_id=(far, d), device_id_type=MESH)

    pl.semaphore_signal(barrier, inc=1, device_id=(near, d), device_id_type=MESH)

    for there, target in ((has_lo, d - 1), (has_hi, d + 1)):
        @pl.when(there)
        def _():
            pl.semaphore_signal(barrier, inc=1, device_id=(r, target), device_id_type=MESH)

    for copy in loads:
        copy.start()

    zero_row = jnp.zeros(u.shape[1:], jnp.float32)
    u[far_slot] = zero_row
    m[far_slot] = zero_row

    @pl.when(jnp.logical_not(has_far))
    def _():
        far_u[...] = zero_row
        far_m[...] = zero_row
        f[far_slot] = zero_row

    @pl.when(jnp.logical_not(has_lo))
    def _():
        lo[...] = jnp.zeros_like(lo)
        lo_b[...] = jnp.zeros_like(lo_b)

    @pl.when(jnp.logical_not(has_hi))
    def _():
        hi[...] = jnp.zeros_like(hi)
        hi_b[...] = jnp.zeros_like(hi_b)

    for copy in loads:
        copy.wait()

    k = diff[b].astype(jnp.float32)
    speed = vel[0, b].astype(jnp.float32)
    coef[...] = TIME_STEP * (
        k + jnp.where(core == 1, -jnp.minimum(speed, 0.0), jnp.maximum(speed, 0.0))
    )

    def edges(i, stage, value):
        edge_lo[stage, i] = value[:1]
        edge_hi[stage, i] = value[-1:]

    def field_edges(i, carry):
        edges(i, 0, u[i + 1])
        return carry

    lax.fori_loop(0, count, field_edges, 0)

    pl.semaphore_wait(barrier, 1 + sum(x.astype(jnp.int32) for x in (has_far, has_lo, has_hi)))

    def remote(name, src, dst, target):
        return pltpu.make_async_remote_copy(
            src_ref=src, dst_ref=dst, send_sem=send.at[name], recv_sem=recv.at[name],
            device_id=target, device_id_type=MESH,
        )

    deep, wide = u.shape[1] // 2, u.shape[2] // SPLIT
    chunk = [
        (pl.ds(deep * p, deep), pl.ds(wide * q, wide)) for q in range(SPLIT) for p in range(2)
    ]
    far_copies = {}
    for h, at in enumerate(chunk):
        for name, src, dst in (
            (FAR_U, u.at[(b + 1,) + at], far_u.at[at]),
            (FAR_M, m.at[(b + 1,) + at], far_m.at[at]),
            (FAR_F, f.at[(b + 1,) + at], f.at[((count + 1) * (1 - core),) + at]),
        ):
            far_copies[name + h] = remote(name + h, src, dst, (far, d))
    near_slot = (count + 1) * core
    near_copies = {
        name: remote(name, ref.at[near_row + 1], ref.at[near_slot], (near, d))
        for name, ref in ((NEAR_U, u), (NEAR_M, m), (NEAR_F, f))
    }
    lo_copies = {
        name: remote(name, src, dst, (r, d - 1))
        for name, src, dst in (
            (LO_U, edge_lo.at[0], hi.at[0]), (LO_M, edge_lo.at[1], hi.at[1]),
            (LO_F, edge_lo.at[2], hi.at[2]), (LO_MB, edge_lo_b.at[0, 0], hi_b.at[0, 0]),
            (LO_FB, edge_lo_b.at[1], hi_b.at[1]),
        )
    }
    hi_copies = {
        name: remote(name, src, dst, (r, d + 1))
        for name, src, dst in (
            (HI_U, edge_hi.at[0], lo.at[0]), (HI_M, edge_hi.at[1], lo.at[1]),
            (HI_F, edge_hi.at[2], lo.at[2]), (HI_MB, edge_hi_b.at[0, 0], lo_b.at[0, 0]),
            (HI_FB, edge_hi_b.at[1], lo_b.at[1]),
        )
    }

    started = {}

    def start_far(name):
        started[name] = far_copies[name], has_far

        @pl.when(has_far)
        def _():
            far_copies[name].start()

    def wait_far(name):
        @pl.when(has_far)
        def _():
            far_copies[name].wait_recv()

    def start_near(name):
        started[name] = near_copies[name], None
        near_copies[name].start()

    def wait_near(name):
        near_copies[name].wait_recv()

    def start_deep(to_lo=None, to_hi=None):
        if to_lo is not None:
            started[to_lo] = lo_copies[to_lo], has_lo
            pl.when(has_lo)(lo_copies[to_lo].start)
        if to_hi is not None:
            started[to_hi] = hi_copies[to_hi], has_hi
            pl.when(has_hi)(hi_copies[to_hi].start)

    def wait_deep(to_lo, to_hi):
        pl.when(has_hi)(lo_copies[to_lo].wait_recv)
        pl.when(has_lo)(hi_copies[to_hi].wait_recv)

    start_deep(LO_U, HI_U)
    start_near(NEAR_U)
    for h in range(CHUNKS):
        start_far(FAR_U + h)
    wait_near(NEAR_U)
    wait_deep(LO_U, HI_U)

    def first(i, carry):
        value = section(u, lo.at[0], hi.at[0], diff, vel, i)
        m[i + 1] = value
        edges(i, 1, value)
        return carry

    first(b, 0)

    def forward_middle():
        for h, at in enumerate(chunk):
            wait_far(FAR_U + h)
            here = (b + 1,) + at
            m[here] = m[here] + coef[at] * far_u[at]
            if h == CHUNKS - 1:
                edge_lo_b[0, 0] = m[b + 1, :1]
                edge_hi_b[0, 0] = m[b + 1, u.shape[1] - 1 :]
                start_deep(LO_MB, HI_MB)
            start_far(FAR_M + h)

    def other_rows():
        lax.fori_loop(1 - core, count - core, first, 0)
        start_deep(LO_M, HI_M)
        start_near(NEAR_M)

    pl.when(upper)(other_rows)
    forward_middle()
    pl.when(jnp.logical_not(upper))(other_rows)
    wait_near(NEAR_M)
    wait_deep(LO_M, HI_M)

    def pass_token(way, there, on, onward):
        @pl.when(there)
        def _():
            pl.semaphore_wait(token.at[way], 1)

        @pl.when(on)
        def _():
            pl.semaphore_signal(token.at[way], inc=1, device_id=(r, onward), device_id_type=MESH)

    def line_entered():
        ahead, back = (0, has_lo, has_hi, d + 1), (1, has_hi, has_lo, d - 1)
        for half, order in ((d < depths // 2, (ahead, back)), (d >= depths // 2, (back, ahead))):
            @pl.when(half)
            def _():
                for way in order:
                    pass_token(*way)

    wait_deep(LO_MB, HI_MB)
    lo[1, b] = lo_b[0, 0]
    hi[1, b] = hi_b[0, 0]
    p_row[...] = section(m, lo.at[1], hi.at[1], diff, vel, b)

    def second(i, carry):
        value = section(m, lo.at[1], hi.at[1], diff, vel, i)
        f[i + 1] = value
        edges(i, 2, value)
        return carry

    def pair(p, carry):
        low, high = lo.at[2], hi.at[2]
        one, two = (
            jnp.concatenate(ray_row(f, low, high, 2 * p + q, opacity), axis=0) for q in range(2)
        )
        left = lax.broadcasted_iota(jnp.int32, (4, 128), 1) < 64
        for j in range(tiles):
            x, y = one[:, j * 128 : (j + 1) * 128], two[:, j * 128 : (j + 1) * 128]
            part[2 * j, p] = jnp.where(left, x, pltpu.roll(y, 64, 1))
            part[2 * j + 1, p] = jnp.where(left, pltpu.roll(x, 64, 1), y)
        return carry

    pairs = count // 2
    groups = pl.ds(1 - core, pairs - 1), pl.ds((pairs - 1) * core, 1)

    def spread(stage, k):
        target = lax.rem(d + k, depths)
        return pltpu.make_async_remote_copy(
            src_ref=part.at[target, groups[stage]], dst_ref=comp.at[d, groups[stage]],
            send_sem=send_a.at[stage, k], recv_sem=recv_a.at[stage, d],
            device_id=(r, target), device_id_type=MESH,
        )

    def start_spread(stage):
        def body(k, carry):
            spread(stage, k).start()
            return carry

        lax.fori_loop(1, depths, body, 0)

    def end_spread(stage):
        def body(k, carry):
            source = lax.rem(d + k, depths)
            pltpu.make_async_remote_copy(
                src_ref=part.at[0, groups[stage]], dst_ref=comp.at[source, groups[stage]],
                send_sem=send_a.at[stage, k], recv_sem=recv_a.at[stage, source],
                device_id=(r, source), device_id_type=MESH,
            ).wait_recv()
            return carry

        lax.fori_loop(1, depths, body, 0)

    lax.fori_loop(first_free, first_free + count - 2, second, 0)
    start_deep(LO_F, HI_F)
    start_near(NEAR_F)
    value = section(m, lo.at[1], hi.at[1], diff, vel, inner)
    f[inner + 1] = value
    edge_lo_b[1, 1] = value[:1]
    edge_hi_b[1, 1] = value[-1:]
    pl.when(jnp.logical_not(upper))(line_entered)
    for h, at in enumerate(chunk):
        wait_far(FAR_M + h)
        f[(b + 1,) + at] = p_row[at] + coef[at] * far_m[at]
        start_far(FAR_F + h)
    edge_lo_b[1, 0] = f[b + 1, :1]
    edge_hi_b[1, 0] = f[b + 1, u.shape[1] - 1 :]
    start_deep(LO_FB, HI_FB)
    pl.when(upper)(line_entered)
    wait_near(NEAR_F)
    wait_deep(LO_F, HI_F)
    lax.fori_loop(1 - core, pairs - core, pair, 0)
    start_spread(0)
    front_out[...] = f[1 : count + 1]
    wait_deep(LO_FB, HI_FB)
    for q, i in enumerate((b, inner)):
        lo[2, i] = lo_b[1, q]
        hi[2, i] = hi_b[1, q]
    for h in range(CHUNKS):
        wait_far(FAR_F + h)
    pair((pairs - 1) * core, 0)
    start_spread(1)
    comp[d] = part[d]

    def composite(p, carry):
        total = jnp.zeros((3, 128), jnp.float32)
        clear = jnp.ones((1, 128), jnp.float32)
        for s in range(depths):
            block = comp[s, p]
            total = total + clear * block[:3]
            clear = clear * block[3:]
        result[p] = jnp.concatenate([total, clear], axis=0)
        return carry

    end_spread(0)
    lax.fori_loop(1 - core, pairs - core, composite, 0)
    end_spread(1)
    composite((pairs - 1) * core, 0)
    for p in range(pairs):
        tile = result[p]
        other = pltpu.roll(tile, 64, 1)
        for v in range(4):
            picture[v, 2 * p : 2 * p + 1] = tile[v : v + 1, :64]
            picture[v, 2 * p + 1 : 2 * p + 2] = other[v : v + 1, :64]

    for copy, there in started.values():
        if there is None:
            copy.wait_send()
        else:
            pl.when(there)(copy.wait_send)

    def sent(k, carry):
        for stage in range(2):
            spread(stage, k).wait_send()
        return carry

    lax.fori_loop(1, depths, sent, 0)

def shards(rows, depths, field, diffusivity, velocity):
    count, deep, width = field.shape
    row = (deep, width)
    f32 = jnp.float32
    pairs = count // 2
    any_space = pl.BlockSpec(memory_space=pl.ANY)
    vmem = pltpu.VMEM
    return pl.pallas_call(
        functools.partial(kernel, rows, depths, OPACITY_TOTAL / (deep * depths)),
        out_shape=(
            pltpu.VMEM(field.shape, f32),
            pltpu.VMEM((4, count, width // depths), f32),
        ),
        in_specs=[any_space] * 3,
        out_specs=(pl.BlockSpec(memory_space=pltpu.VMEM), pl.BlockSpec(memory_space=pltpu.VMEM)),
        scratch_shapes=[
            vmem((count + 2,) + row, f32),
            vmem((count + 2,) + row, f32),
            vmem((count + 2,) + row, f32),
            vmem(diffusivity.shape, diffusivity.dtype),
            vmem(velocity.shape, velocity.dtype),
            vmem(row, f32), vmem(row, f32), vmem(row, f32), vmem(row, f32),
            vmem((3, count, 1, width), f32), vmem((3, count, 1, width), f32),
            vmem((3, count, 1, width), f32), vmem((3, count, 1, width), f32),
            vmem((2, 2, 1, width), f32), vmem((2, 2, 1, width), f32),
            vmem((2, 2, 1, width), f32), vmem((2, 2, 1, width), f32),
            vmem((depths, pairs, 4, 128), f32),
            vmem((depths, pairs, 4, 128), f32),
            vmem((pairs, 4, 128), f32),
            pltpu.SemaphoreType.DMA((3,)),
            pltpu.SemaphoreType.DMA((COPIES,)),
            pltpu.SemaphoreType.DMA((COPIES,)),
            pltpu.SemaphoreType.DMA((2, depths)),
            pltpu.SemaphoreType.DMA((2, depths)),
            pltpu.SemaphoreType.REGULAR((2,)),
        ],
        compiler_params=pltpu.CompilerParams(collective_id=0, has_side_effects=True),
        name="front_and_rays",
    )(field, diffusivity, velocity)

def solution(mesh):
    return jax.shard_map(
        functools.partial(shards, mesh.shape["rows"], mesh.shape["depth"]),
        mesh=mesh,
        in_specs=(
            P("rows", "depth", None),
            P("rows", "depth", None),
            P(None, "rows", "depth", None),
        ),
        out_specs=(P("rows", "depth", None), P(None, "rows", "depth")),
        check_vma=False,
    )
```

```python
import functools

import jax
import jax.numpy as jnp
from jax import lax
from jax.experimental import pallas as pl
from jax.experimental.pallas import tpu as pltpu
from jax.sharding import PartitionSpec as P

TIME_STEP = 0.2
OPACITY_TOTAL = 3.0
MESH = pl.DeviceIdType.MESH

(NEAR_U, LO_U, HI_U, NEAR_M, LO_M, HI_M, NEAR_F, LO_F, HI_F,
 LO_MB, HI_MB, LO_FB, HI_FB, FAR_U) = range(14)
SPLIT = 4
CHUNKS = 2 * SPLIT
FAR_M, FAR_F = FAR_U + CHUNKS, FAR_U + 2 * CHUNKS
FAR_C = FAR_U + 3 * CHUNKS
FAR_P, COPIES = FAR_C + 1, FAR_C + 2

def shifted(value, before, axis, low, high):
    size = value.shape[axis]
    index = lax.broadcasted_iota(jnp.int32, value.shape, axis)
    if before:
        return jnp.where(index == 0, low, pltpu.roll(value, 1, axis))
    return jnp.where(index == size - 1, high, pltpu.roll(value, size - 1, axis))

def section(ref, low, high, diff, vel, i):
    center, row_before, row_after = ref[i + 1], ref[i], ref[i + 2]
    deep_before = shifted(center, True, 0, low[i], None)
    deep_after = shifted(center, False, 0, None, high[i])
    col_before = shifted(center, True, 1, 0.0, None)
    col_after = shifted(center, False, 1, None, 0.0)
    k = diff[i].astype(jnp.float32)
    total = 1.0 - 6.0 * k
    flow = None
    for dim, (back, ahead) in enumerate(
        ((row_before, row_after), (deep_before, deep_after), (col_before, col_after))
    ):
        speed = vel[dim, i].astype(jnp.float32)
        up, down = jnp.maximum(speed, 0.0), jnp.minimum(speed, 0.0)
        part = (k + up) * back + (k - down) * ahead
        flow = part if flow is None else flow + part
        total = total - (up - down)
    return center + TIME_STEP * (flow + center * (total - center))

def ray_row(ref, low, high, i, opacity):
    center = ref[i + 1]
    grad_row = (ref[i + 2] - ref[i]) * 0.5
    grad_deep = (shifted(center, False, 0, None, high[i]) - shifted(center, True, 0, low[i], None)) * 0.5
    grad_col = (shifted(center, False, 1, None, 0.0) - shifted(center, True, 1, 0.0, None)) * 0.5
    lighting = 0.48 * grad_row + 0.64 * grad_deep + 0.6 * grad_col
    magnitude = grad_row * grad_row + grad_deep * grad_deep + grad_col * grad_col + 0.1
    shade = 0.35 + 0.65 * lighting * lighting / magnitude
    optical = opacity * center
    size = center.shape[0]
    index = lax.broadcasted_iota(jnp.int32, center.shape, 0)
    through, step = optical, 1
    while step < size:
        through = through + jnp.where(index >= step, pltpu.roll(through, step, 0), 0.0)
        step *= 2
    weight = jnp.exp(optical - through) * (1.0 - jnp.exp(-optical)) * shade
    bright = weight * center
    red = jnp.sum(bright, axis=0, keepdims=True)
    green = jnp.sum(bright * center, axis=0, keepdims=True)
    blue = jnp.sum(weight - bright, axis=0, keepdims=True)
    return red, green, blue, jnp.exp(-through[size - 1 : size])

def kernel(rows, depths, opacity, field, diffusivity, velocity, front_out, picture, u, m, f, diff,
           vel, coef, far_u, far_c, far_m, far_p, p_row, lo, hi, edge_lo, edge_hi, lo_b, hi_b,
           edge_lo_b, edge_hi_b, part, comp, result, load, send, recv, send_a, recv_a, token):
    r, d = lax.axis_index("rows"), lax.axis_index("depth")
    core = r % 2
    count = field.shape[0]
    last = count - 1
    b = last * core
    inner = last - 1 - (last - 2) * (1 - core)
    near_row = last - b
    far_slot = (count + 1) * core
    first_free = 2 * (1 - core)
    near, far = r + 1 - 2 * core, r - 1 + 2 * core
    has_far = jnp.logical_and(far >= 0, far < rows)
    has_lo, has_hi = d > 0, d < depths - 1
    whole = jnp.logical_and(has_far, d < 5 * depths // 8)
    terms = jnp.logical_and(has_far, d >= 5 * depths // 8)
    upper = r // 2 % 2 == 1
    tiles = field.shape[2] // 128

    loads = [
        pltpu.make_async_copy(field, u.at[pl.ds(1, count)], load.at[0]),
        pltpu.make_async_copy(diffusivity, diff, load.at[1]),
        pltpu.make_async_copy(velocity, vel, load.at[2]),
    ]
    barrier = pltpu.get_barrier_semaphore()

    @pl.when(has_far)
    def _():
        pl.semaphore_signal(barrier, inc=1, device_id=(far, d), device_id_type=MESH)

    pl.semaphore_signal(barrier, inc=1, device_id=(near, d), device_id_type=MESH)

    for there, target in ((has_lo, d - 1), (has_hi, d + 1)):
        @pl.when(there)
        def _():
            pl.semaphore_signal(barrier, inc=1, device_id=(r, target), device_id_type=MESH)

    for copy in loads:
        copy.start()

    zero_row = jnp.zeros(u.shape[1:], jnp.float32)
    u[far_slot] = zero_row
    m[far_slot] = zero_row

    @pl.when(jnp.logical_not(has_far))
    def _():
        far_u[...] = zero_row
        far_m[...] = zero_row
        f[far_slot] = zero_row

    @pl.when(jnp.logical_not(has_lo))
    def _():
        lo[...] = jnp.zeros_like(lo)
        lo_b[...] = jnp.zeros_like(lo_b)

    @pl.when(jnp.logical_not(has_hi))
    def _():
        hi[...] = jnp.zeros_like(hi)
        hi_b[...] = jnp.zeros_like(hi_b)

    for copy in loads:
        copy.wait()

    k = diff[b].astype(jnp.float32)
    speed = vel[0, b].astype(jnp.float32)
    coef[...] = TIME_STEP * (
        k + jnp.where(core == 1, -jnp.minimum(speed, 0.0), jnp.maximum(speed, 0.0))
    )

    def edges(i, stage, value):
        edge_lo[stage, i] = value[:1]
        edge_hi[stage, i] = value[-1:]

    def field_edges(i, carry):
        edges(i, 0, u[i + 1])
        return carry

    lax.fori_loop(0, count, field_edges, 0)

    pl.semaphore_wait(barrier, 1 + sum(x.astype(jnp.int32) for x in (has_far, has_lo, has_hi)))

    def remote(name, src, dst, target):
        return pltpu.make_async_remote_copy(
            src_ref=src, dst_ref=dst, send_sem=send.at[name], recv_sem=recv.at[name],
            device_id=target, device_id_type=MESH,
        )

    deep, wide = u.shape[1] // 2, u.shape[2] // SPLIT
    chunk = [
        (pl.ds(deep * p, deep), pl.ds(wide * q, wide)) for q in range(SPLIT) for p in range(2)
    ]
    far_copies = {
        FAR_C: remote(FAR_C, coef, far_c, (far, d)),
        FAR_P: remote(FAR_P, p_row, far_p, (far, d)),
    }
    for h, at in enumerate(chunk):
        for name, src, dst in (
            (FAR_U, u.at[(b + 1,) + at], far_u.at[at]),
            (FAR_M, m.at[(b + 1,) + at], far_m.at[at]),
            (FAR_F, f.at[(b + 1,) + at], f.at[((count + 1) * (1 - core),) + at]),
        ):
            far_copies[name + h] = remote(name + h, src, dst, (far, d))
    near_slot = (count + 1) * core
    near_copies = {
        name: remote(name, ref.at[near_row + 1], ref.at[near_slot], (near, d))
        for name, ref in ((NEAR_U, u), (NEAR_M, m), (NEAR_F, f))
    }
    lo_copies = {
        name: remote(name, src, dst, (r, d - 1))
        for name, src, dst in (
            (LO_U, edge_lo.at[0], hi.at[0]), (LO_M, edge_lo.at[1], hi.at[1]),
            (LO_F, edge_lo.at[2], hi.at[2]), (LO_MB, edge_lo_b.at[0, 0], hi_b.at[0, 0]),
            (LO_FB, edge_lo_b.at[1], hi_b.at[1]),
        )
    }
    hi_copies = {
        name: remote(name, src, dst, (r, d + 1))
        for name, src, dst in (
            (HI_U, edge_hi.at[0], lo.at[0]), (HI_M, edge_hi.at[1], lo.at[1]),
            (HI_F, edge_hi.at[2], lo.at[2]), (HI_MB, edge_hi_b.at[0, 0], lo_b.at[0, 0]),
            (HI_FB, edge_hi_b.at[1], lo_b.at[1]),
        )
    }

    started = {}

    def start_far(name, there=has_far):
        started[name] = far_copies[name], there
        pl.when(there)(far_copies[name].start)

    def wait_far(name, there=has_far):
        pl.when(there)(far_copies[name].wait_recv)

    def start_near(name):
        started[name] = near_copies[name], None
        near_copies[name].start()

    def wait_near(name):
        near_copies[name].wait_recv()

    def start_deep(to_lo=None, to_hi=None):
        if to_lo is not None:
            started[to_lo] = lo_copies[to_lo], has_lo
            pl.when(has_lo)(lo_copies[to_lo].start)
        if to_hi is not None:
            started[to_hi] = hi_copies[to_hi], has_hi
            pl.when(has_hi)(hi_copies[to_hi].start)

    def wait_deep(to_lo, to_hi):
        pl.when(has_hi)(lo_copies[to_lo].wait_recv)
        pl.when(has_lo)(hi_copies[to_hi].wait_recv)

    start_deep(LO_U, HI_U)
    start_near(NEAR_U)
    for h in range(CHUNKS):
        start_far(FAR_U + h)
    wait_near(NEAR_U)
    wait_deep(LO_U, HI_U)
    start_far(FAR_C, terms)

    def first(i, carry):
        value = section(u, lo.at[0], hi.at[0], diff, vel, i)
        m[i + 1] = value
        edges(i, 1, value)
        return carry

    first(b, 0)

    def forward_middle():
        for h, at in enumerate(chunk):
            wait_far(FAR_U + h)
            here = (b + 1,) + at
            m[here] = m[here] + coef[at] * far_u[at]
            if h == CHUNKS - 1:
                edge_lo_b[0, 0] = m[b + 1, :1]
                edge_hi_b[0, 0] = m[b + 1, u.shape[1] - 1 :]
                start_deep(LO_MB, HI_MB)
            start_far(FAR_M + h)

    def other_rows():
        lax.fori_loop(1 - core, count - core, first, 0)
        start_deep(LO_M, HI_M)
        start_near(NEAR_M)

    pl.when(upper)(other_rows)
    forward_middle()
    pl.when(jnp.logical_not(upper))(other_rows)
    wait_near(NEAR_M)
    wait_deep(LO_M, HI_M)

    def pass_token(way, there, on, onward):
        @pl.when(there)
        def _():
            pl.semaphore_wait(token.at[way], 1)

        @pl.when(on)
        def _():
            pl.semaphore_signal(token.at[way], inc=1, device_id=(r, onward), device_id_type=MESH)

    def line_entered():
        ahead, back = (0, has_lo, has_hi, d + 1), (1, has_hi, has_lo, d - 1)
        for half, order in ((d < depths // 2, (ahead, back)), (d >= depths // 2, (back, ahead))):
            @pl.when(half)
            def _():
                for way in order:
                    pass_token(*way)

    wait_deep(LO_MB, HI_MB)
    lo[1, b] = lo_b[0, 0]
    hi[1, b] = hi_b[0, 0]
    p_row[...] = section(m, lo.at[1], hi.at[1], diff, vel, b)
    start_far(FAR_P, terms)

    def second(i, carry):
        value = section(m, lo.at[1], hi.at[1], diff, vel, i)
        f[i + 1] = value
        edges(i, 2, value)
        return carry

    def pair(p, carry):
        low, high = lo.at[2], hi.at[2]
        one, two = (
            jnp.concatenate(ray_row(f, low, high, 2 * p + q, opacity), axis=0) for q in range(2)
        )
        left = lax.broadcasted_iota(jnp.int32, (4, 128), 1) < 64
        for j in range(tiles):
            x, y = one[:, j * 128 : (j + 1) * 128], two[:, j * 128 : (j + 1) * 128]
            part[2 * j, p] = jnp.where(left, x, pltpu.roll(y, 64, 1))
            part[2 * j + 1, p] = jnp.where(left, pltpu.roll(x, 64, 1), y)
        return carry

    pairs = count // 2
    groups = pl.ds(1 - core, pairs - 1), pl.ds((pairs - 1) * core, 1)

    def spread(stage, k):
        target = lax.rem(d + k, depths)
        return pltpu.make_async_remote_copy(
            src_ref=part.at[target, groups[stage]], dst_ref=comp.at[d, groups[stage]],
            send_sem=send_a.at[stage, k], recv_sem=recv_a.at[stage, d],
            device_id=(r, target), device_id_type=MESH,
        )

    def start_spread(stage):
        def body(k, carry):
            spread(stage, k).start()
            return carry

        lax.fori_loop(1, depths, body, 0)

    def end_spread(stage):
        def body(k, carry):
            source = lax.rem(d + k, depths)
            pltpu.make_async_remote_copy(
                src_ref=part.at[0, groups[stage]], dst_ref=comp.at[source, groups[stage]],
                send_sem=send_a.at[stage, k], recv_sem=recv_a.at[stage, source],
                device_id=(r, source), device_id_type=MESH,
            ).wait_recv()
            return carry

        lax.fori_loop(1, depths, body, 0)

    lax.fori_loop(first_free, first_free + count - 2, second, 0)
    start_deep(LO_F, HI_F)
    start_near(NEAR_F)
    value = section(m, lo.at[1], hi.at[1], diff, vel, inner)
    f[inner + 1] = value
    edge_lo_b[1, 1] = value[:1]
    edge_hi_b[1, 1] = value[-1:]
    pl.when(jnp.logical_not(upper))(line_entered)
    for h, at in enumerate(chunk):
        wait_far(FAR_M + h)
        f[(b + 1,) + at] = p_row[at] + coef[at] * far_m[at]
        start_far(FAR_F + h, whole)
    edge_lo_b[1, 0] = f[b + 1, :1]
    edge_hi_b[1, 0] = f[b + 1, u.shape[1] - 1 :]
    start_deep(LO_FB, HI_FB)
    pl.when(upper)(line_entered)
    wait_near(NEAR_F)
    wait_deep(LO_F, HI_F)
    lax.fori_loop(1 - core, pairs - core, pair, 0)
    start_spread(0)
    front_out[...] = f[1 : count + 1]
    wait_deep(LO_FB, HI_FB)
    for q, i in enumerate((b, inner)):
        lo[2, i] = lo_b[1, q]
        hi[2, i] = hi_b[1, q]
    for h in range(CHUNKS):
        wait_far(FAR_F + h, whole)
    wait_far(FAR_C, terms)
    wait_far(FAR_P, terms)

    @pl.when(terms)
    def _():
        f[far_slot] = far_p[...] + far_c[...] * m[b + 1]

    pair((pairs - 1) * core, 0)
    start_spread(1)
    comp[d] = part[d]

    def composite(p, carry):
        total = jnp.zeros((3, 128), jnp.float32)
        clear = jnp.ones((1, 128), jnp.float32)
        for s in range(depths):
            block = comp[s, p]
            total = total + clear * block[:3]
            clear = clear * block[3:]
        result[p] = jnp.concatenate([total, clear], axis=0)
        return carry

    end_spread(0)
    lax.fori_loop(1 - core, pairs - core, composite, 0)
    end_spread(1)
    composite((pairs - 1) * core, 0)
    for p in range(pairs):
        tile = result[p]
        other = pltpu.roll(tile, 64, 1)
        for v in range(4):
            picture[v, 2 * p : 2 * p + 1] = tile[v : v + 1, :64]
            picture[v, 2 * p + 1 : 2 * p + 2] = other[v : v + 1, :64]

    for copy, there in started.values():
        if there is None:
            copy.wait_send()
        else:
            pl.when(there)(copy.wait_send)

    def sent(k, carry):
        for stage in range(2):
            spread(stage, k).wait_send()
        return carry

    lax.fori_loop(1, depths, sent, 0)

def shards(rows, depths, field, diffusivity, velocity):
    count, deep, width = field.shape
    row = (deep, width)
    f32 = jnp.float32
    pairs = count // 2
    any_space = pl.BlockSpec(memory_space=pl.ANY)
    vmem = pltpu.VMEM
    return pl.pallas_call(
        functools.partial(kernel, rows, depths, OPACITY_TOTAL / (deep * depths)),
        out_shape=(
            pltpu.VMEM(field.shape, f32),
            pltpu.VMEM((4, count, width // depths), f32),
        ),
        in_specs=[any_space] * 3,
        out_specs=(pl.BlockSpec(memory_space=pltpu.VMEM), pl.BlockSpec(memory_space=pltpu.VMEM)),
        scratch_shapes=[
            vmem((count + 2,) + row, f32),
            vmem((count + 2,) + row, f32),
            vmem((count + 2,) + row, f32),
            vmem(diffusivity.shape, diffusivity.dtype),
            vmem(velocity.shape, velocity.dtype),
            vmem(row, f32), vmem(row, f32), vmem(row, f32), vmem(row, f32), vmem(row, f32), vmem(row, f32),
            vmem((3, count, 1, width), f32), vmem((3, count, 1, width), f32),
            vmem((3, count, 1, width), f32), vmem((3, count, 1, width), f32),
            vmem((2, 2, 1, width), f32), vmem((2, 2, 1, width), f32),
            vmem((2, 2, 1, width), f32), vmem((2, 2, 1, width), f32),
            vmem((depths, pairs, 4, 128), f32),
            vmem((depths, pairs, 4, 128), f32),
            vmem((pairs, 4, 128), f32),
            pltpu.SemaphoreType.DMA((3,)),
            pltpu.SemaphoreType.DMA((COPIES,)),
            pltpu.SemaphoreType.DMA((COPIES,)),
            pltpu.SemaphoreType.DMA((2, depths)),
            pltpu.SemaphoreType.DMA((2, depths)),
            pltpu.SemaphoreType.REGULAR((2,)),
        ],
        compiler_params=pltpu.CompilerParams(collective_id=0, has_side_effects=True),
        name="front_and_rays",
    )(field, diffusivity, velocity)

def solution(mesh):
    return jax.shard_map(
        functools.partial(shards, mesh.shape["rows"], mesh.shape["depth"]),
        mesh=mesh,
        in_specs=(
            P("rows", "depth", None),
            P("rows", "depth", None),
            P(None, "rows", "depth", None),
        ),
        out_specs=(P("rows", "depth", None), P(None, "rows", "depth")),
        check_vma=False,
    )
```
